32 devices in a mesh: tm: 8 (over z, x), space: 4 (over y, core).
Axes of the slice: x: 2, y: 2, z: 4, core: 2. Of those that a mesh axis runs over, the one named last changes fastest.
Arguments:
- sources: float32 [16, 4, 512, 256], P('tm', None, 'space'), may hold values from -36 to 36
- starts: float32 [16, 512, 256], P('tm', 'space'), may hold values from -24 to 24
- coupling: float32 [512], P('space'), may hold values from 0.05 to 0.25
- classes: int32 [512, 2], P('space'), may hold values from 0 to 3
- inverses: float32 [4, 128, 128], replicated, may hold values from 0 to 1
- coarse_rate: float32 [4, 128], replicated, may hold values from 0.002 to 0.5
Outputs:
- states: float32 [16, 4, 512, 256], P('tm', None, 'space')
The draws below stay inside these ranges and needn't reach their ends.
All inputs are finite; a program needn't handle non-finite values.
Results may differ from the reference program's by a relative error of at most 0.0003.
Values sent between devices are 32-bit elements; how exact they have to be, the bound alone decides.
A program may use at most 64 MiB of HBM per device.

```python
import math
import jax
import jax.numpy as jnp
from jax import lax

LB = 128
BLOCKS = 2
STEPS = 4
CLASSES = 4
LINE = 256
ROWS = 512
GROUPS = 16


def draw_inverses(key, part):
    first_key, second_key = jax.random.split(jax.random.fold_in(key, 17))
    cond_lo, cond_hi, leak_lo, leak_hi = (150.0, 1500.0, 0.01, 0.1)
    conduct = jnp.exp(jax.random.uniform(first_key, (CLASSES, LB - 1), jnp.float32, jnp.log(cond_lo), jnp.log(cond_hi)))
    leakage = jnp.exp(jax.random.uniform(second_key, (CLASSES, LB), jnp.float32, jnp.log(leak_lo), jnp.log(leak_hi)))
    left_side = jnp.pad(conduct, ((0, 0), (1, 0)))
    right_side = jnp.pad(conduct, ((0, 0), (0, 1)))
    diagonal = 1.5 + leakage + left_side + right_side
    identity = jnp.eye(LB, dtype=jnp.float32)
    upper = jnp.eye(LB, k=1, dtype=jnp.float32)
    lower = jnp.eye(LB, k=-1, dtype=jnp.float32)
    matrix = diagonal[:, :, None] * identity - right_side[:, :, None] * upper - left_side[:, :, None] * lower
    return jnp.linalg.inv(matrix).astype(jnp.float32)


def place_ends(entries, key, least, high):
    extent = entries.shape
    place = [jax.random.randint(jax.random.fold_in(key, axis), (), 0, extent[axis]) for axis in range(len(extent))]
    entries = entries.at[tuple(place)].set(least)
    longest = extent.index(max(extent))
    place[longest] = (place[longest] + 1) % extent[longest]
    return entries.at[tuple(place)].set(high)


def steps_of(own_key, dims, cuts, low, high):
    factor_of, own = 1.0, jax.random.fold_in(own_key, 6)
    for dim, shards_of in cuts:
        steps = jnp.exp(jax.random.uniform(jax.random.fold_in(own, dim), (shards_of,), jnp.float32, low / len(cuts), high / len(cuts)))
        factor_of = factor_of * jnp.repeat(steps, dims[dim] // shards_of).reshape([-1 if axis == dim else 1 for axis in range(len(dims))])
    return factor_of


def noise(stream_key, shape, scale, limit, cuts=(), held_as=jnp.bfloat16):
    array = scale * jax.random.normal(stream_key, shape, jnp.float32)
    if cuts:
        array = array * steps_of(stream_key, shape, cuts, -0.22, 0.18)
    return jnp.clip(array, -limit, limit).astype(held_as)


def setup_inputs(seed: int = 0) -> dict:
    arg_keys = jax.random.split(jax.random.key(seed), 7)
    return {
        "sources": noise(arg_keys[0], (GROUPS, STEPS, ROWS, LINE), 6.0, 36.0, ((0, 8), (2, 4)), jnp.float32),
        "starts": noise(arg_keys[1], (GROUPS, ROWS, LINE), 4.0, 24.0, ((0, 8), (1, 4)), jnp.float32),
        "coupling": jnp.clip(0.05 + 0.2 * jax.random.uniform(arg_keys[2], (ROWS,), jnp.float32) ** steps_of(arg_keys[2], (ROWS,), ((0, 4),), -0.2, 0.2), 0.05, 0.25),
        "classes": place_ends(jax.random.randint(arg_keys[3], (ROWS, BLOCKS), 0, CLASSES), jax.random.fold_in(arg_keys[3], 1), 0, CLASSES - 1).astype(jnp.int32),
        "inverses": draw_inverses(jax.random.fold_in(arg_keys[6], 71), 0),
        "coarse_rate": jnp.clip(jnp.exp(jax.random.uniform(arg_keys[5], (CLASSES, LB), jnp.float32, math.log(0.002), math.log(0.5))), 0.002, 0.5),
    }


def advance(field, source, coupling, table):
    padded = jnp.pad(field, ((0, 0), (1, 1), (0, 0)))
    rhs = field + coupling[None, :, None] * (padded[:, :-2] + padded[:, 2:]) + source
    group_count, row_count, line_len = rhs.shape
    blocked = rhs.reshape(group_count, row_count, line_len // LB, LB)
    result = jnp.einsum('krbj,rbij->krbi', blocked, table, precision=lax.Precision.HIGHEST)
    return result.reshape(group_count, row_count, line_len)

def reference(sources, starts, coupling, classes, inverses, coarse_rate):
    table = inverses[classes]
    decay = jnp.exp(-coarse_rate[classes]).reshape(ROWS, LINE)
    fine_state = starts
    for substep in range(STEPS - 1):
        fine_state = advance(fine_state, sources[:, substep], coupling, table)
    ends = advance(fine_state, sources[:, STEPS - 1], coupling, table)
    new_starts = jnp.concatenate([starts[:1], ends[:-1]], axis=0)
    fine_state = new_starts
    for substep in range(STEPS - 1):
        fine_state = advance(fine_state, sources[:, substep], coupling, table)
    resid = advance(fine_state, sources[:, STEPS - 1], coupling, table) - ends

    def link(carried, term):
        carried = decay * carried + term
        return (carried, carried)
    _, errors = lax.scan(link, jnp.zeros((ROWS, LINE), jnp.float32), resid)
    finals = ends + errors
    fine_state = jnp.concatenate([starts[:1], finals[:-1]], axis=0)
    collected = []
    for substep in range(STEPS - 1):
        fine_state = advance(fine_state, sources[:, substep], coupling, table)
        collected.append(fine_state)
    collected.append(finals)
    return jnp.stack(collected, axis=1)
```

```python
import functools

import jax
import jax.numpy as jnp
from jax import lax
from jax.experimental import pallas as pl
from jax.experimental.pallas import tpu as pltpu
from jax.sharding import PartitionSpec as P

PAD = 8
CHUNKS = 3
VMEM_LIMIT = 60 * 1024 * 1024
MESH = pl.DeviceIdType.MESH


def ceil8(x):
    return -(-x // 8) * 8


def kernel(cfg, sources, starts, coupling, classes, inverses, rate, out,
           F, S, CPH, CLH, CP, MK, OD, W, FIN, ENDS, RES, DEC, R, RP, EI, EP, EN, FW, DL, OB,
           in_sem, hs, hr, es, er, rs, rr, fs, fr, ps, pr, out_sem):
    tm, space = cfg
    G, RL, L = starts.shape
    steps = sources.shape[1]
    C, LB, _ = inverses.shape
    B = L // LB
    KH = C // 2
    T = 3 * steps - 1
    HM = ceil8(T)
    HB = ceil8(T - steps)
    NB = RL + 2 * HB
    HALF = NB // 2
    CH = HALF // CHUNKS
    f32, bf16 = jnp.float32, jnp.bfloat16
    t = lax.axis_index("tm")
    s = lax.axis_index("space")
    p = lax.rem(t, 2)
    partner = t + 1 - 2 * p
    has_up, has_dn = s > 0, s < space - 1
    has_prev, has_next = t > 0, t < tm - 1
    has_pz, has_nz = t > 1, t < tm - 2

    own = pl.ds(HM, RL)
    in_starts = pltpu.make_async_copy(starts, F.at[:, pl.ds(PAD + HM, RL), :], in_sem.at[0])
    in_starts.start()
    in_src = [
        pltpu.make_async_copy(sources.at[:, m], S.at[:, m, own, :], in_sem.at[1 + m])
        for m in range(steps)
    ]
    for c in in_src:
        c.start()

    barrier = pltpu.get_barrier_semaphore()
    peers = [
        (has_up, (t, s - 1)), (has_dn, (t, s + 1)),
        (has_prev, (t - 1, s)), (has_next, (t + 1, s)),
        (has_pz, (t - 2, s)), (has_nz, (t + 2, s)),
    ]
    for cond, dev in peers:
        @pl.when(cond)
        def _(dev=dev):
            pl.semaphore_signal(barrier, inc=1, device_id=dev, device_id_type=MESH)
    pl.semaphore_wait(barrier, sum(jnp.where(cond, 1, 0) for cond, _ in peers))

    def remote(src, dst, a, b, dev):
        return pltpu.make_async_remote_copy(
            src_ref=src, dst_ref=dst, send_sem=a, recv_sem=b, device_id=dev, device_id_type=MESH
        )

    down, up = [], []
    halves = [HM if T - (m + 1) > HM - 8 else ceil8(T - (m + 1)) for m in range(steps)]
    down.append((coupling, CPH.at[0]))
    up.append((coupling, CPH.at[1]))
    down.append((classes, CLH.at[0]))
    up.append((classes, CLH.at[1]))
    down.append((starts.at[:, pl.ds(RL - HM, HM), :], F.at[:, pl.ds(PAD, HM), :]))
    up.append((starts.at[:, pl.ds(0, HM), :], F.at[:, pl.ds(PAD + HM + RL, HM), :]))
    for m in range(steps):
        h = halves[m]
        down.append((sources.at[:, m, pl.ds(RL - h, h), :], S.at[:, m, pl.ds(HM - h, h), :]))
        up.append((sources.at[:, m, pl.ds(0, h), :], S.at[:, m, pl.ds(HM + RL, h), :]))
    n_halo = len(down)
    down = [remote(a, b, hs.at[0, i], hr.at[0, i], (t, s + 1)) for i, (a, b) in enumerate(down)]
    up = [remote(a, b, hs.at[1, i], hr.at[1, i], (t, s - 1)) for i, (a, b) in enumerate(up)]

    @pl.when(has_dn)
    def _():
        for c in down:
            c.start()

    @pl.when(has_up)
    def _():
        for c in up:
            c.start()

    def clear(side):
        CPH[side] = jnp.zeros(CPH.shape[1:], f32)
        CLH[side] = jnp.zeros(CLH.shape[1:], jnp.int32)
        F[:, pl.ds(PAD + side * (HM + RL), HM), :] = jnp.zeros((G, HM, L), f32)
        S[:, :, pl.ds(side * (HM + RL), HM), :] = jnp.zeros((G, steps, HM, L), f32)

    @pl.when(jnp.logical_not(has_up))
    def _():
        clear(0)

    @pl.when(jnp.logical_not(has_dn))
    def _():
        clear(1)

    for g in range(G):
        F[g, pl.ds(0, PAD), :] = jnp.zeros((PAD, L), f32)
        F[g, pl.ds(PAD + HM * 2 + RL, PAD), :] = jnp.zeros((PAD, L), f32)

    for k in range(KH):
        for o in range(2):
            wt = inverses[2 * k + o].T
            hi = wt.astype(bf16)
            lo = (wt - hi.astype(f32)).astype(bf16)
            cols = pl.ds(o * LB, LB)
            W[pl.ds(k * LB, LB), cols] = hi
            W[pl.ds((KH + k) * LB, LB), cols] = hi
            W[pl.ds((2 * KH + k) * LB, LB), cols] = lo

    def column(row):
        return jnp.broadcast_to(row, (LB, RL)).T

    def fields(row, cls, part, n):
        for b in range(B):
            cl = column(cls[b : b + 1, :].astype(f32))[part]
            for k in range(KH):
                MK[b, k, pl.ds(row, n), :] = jnp.where((cl == 2 * k) | (cl == 2 * k + 1), 1.0, 0.0).astype(bf16)
            odd = cl == 1
            for k in range(1, KH):
                odd = odd | (cl == 2 * k + 1)
            OD[b, pl.ds(row, n), :] = jnp.where(odd, 1.0, 0.0)
            r = jnp.broadcast_to(rate[0:1, :], (n, LB))
            for c in range(1, C):
                r = jnp.where(cl == c, jnp.broadcast_to(rate[c : c + 1, :], (n, LB)), r)
            DEC[pl.ds(row, n), pl.ds(b * LB, LB)] = jnp.exp(-r)

    CP[own, :] = column(coupling[...])
    fields(HM, classes[...], slice(0, RL), RL)

    @pl.when(has_up)
    def _():
        for c in down:
            c.wait_recv()

    @pl.when(has_dn)
    def _():
        for c in up:
            c.wait_recv()

    CP[pl.ds(0, HM), :] = column(CPH[0])[RL - HM :]
    CP[pl.ds(HM + RL, HM), :] = column(CPH[1])[:HM]
    fields(0, CLH[0], slice(RL - HM, RL), HM)
    fields(HM + RL, CLH[1], slice(0, HM), HM)

    in_starts.wait()
    for c in in_src:
        c.wait()

    big = pl.ds(HM - HB, NB)
    fbig = pl.ds(PAD + HM - HB, NB)

    @pl.when(jnp.logical_not(has_prev))
    def _():
        FIN[...] = F[0, fbig, :]

    def phi(g, m, t_step):
        h = ceil8(T - t_step)
        lo, n = HM - h, RL + 2 * h
        xs = []
        for b in range(B):
            ln = pl.ds(b * LB, LB)
            v = F[g, pl.ds(PAD + lo, n), ln]
            a = F[g, pl.ds(PAD + lo - 1, n), ln]
            d = F[g, pl.ds(PAD + lo + 1, n), ln]
            rhs = v + CP[pl.ds(lo, n), :] * (a + d) + S[g, m, pl.ds(lo, n), ln]
            hi = rhs.astype(bf16)
            low = (rhs - hi.astype(f32)).astype(bf16)
            mk = [MK[b, k, pl.ds(lo, n), :] for k in range(KH)]
            his = [hi * q for q in mk]
            xs.append(jnp.concatenate(his + [low * q for q in mk] + his, axis=1))
        y = jnp.dot(jnp.concatenate(xs, axis=0), W[...], preferred_element_type=f32)
        res = []
        for b in range(B):
            odd = OD[b, pl.ds(lo, n), :] > 0.5
            yb = y[b * n : (b + 1) * n]
            res.append(jnp.where(odd, yb[:, LB:], yb[:, :LB]))
        return jnp.concatenate(res, axis=1), lo, n

    def relax(g, first):
        for m in range(steps - 1):
            res, lo, n = phi(g, m, first + m)
            F[g, pl.ds(PAD + lo, n), :] = res

    send_ends = remote(ENDS.at[G - 1], FIN, es.at[0], er.at[0], (t + 1, s))
    for g in [G - 1] + list(range(G - 1)):
        relax(g, 1)
        res, lo, n = phi(g, steps - 1, steps)
        ENDS[g] = res
        if g == G - 1:
            @pl.when(has_next)
            def _():
                send_ends.start()

    for g in list(range(1, G)) + [0]:
        if g == 0:
            @pl.when(has_prev)
            def _():
                send_ends.wait_recv()
            F[g, fbig, :] = FIN[...]
        else:
            F[g, fbig, :] = ENDS[g - 1]
        relax(g, steps + 1)
        res, lo, n = phi(g, steps - 1, 2 * steps)
        RES[g] = res - ENDS[g]

    dec = DEC[big, :]
    acc = RES[0]
    for g in range(1, G):
        acc = dec * acc + RES[g]
    R[...] = acc
    keep = pl.multiple_of((1 - p) * HALF, 8)
    give = pl.multiple_of(p * HALF, 8)
    swap = remote(R.at[pl.ds(give, HALF), :], RP, rs.at[0], rr.at[0], (partner, s))
    swap.start()

    @pl.when(jnp.logical_not(has_pz))
    def _():
        EI[...] = jnp.zeros((HALF, L), f32)

    chunk = [pl.ds(j * CH, CH) for j in range(CHUNKS)]
    forward = [remote(FW.at[c], EI.at[c], fs.at[j], fr.at[j], (t + 2, s)) for j, c in enumerate(chunk)]
    deliver0 = [remote(DL.at[c], EP.at[c], ps.at[j], pr.at[j], (partner, s)) for j, c in enumerate(chunk)]
    deliver1 = [remote(EI.at[c], EP.at[c], ps.at[j], pr.at[j], (partner, s)) for j, c in enumerate(chunk)]
    swap.wait_recv()
    for j in range(CHUNKS):
        mine = pl.ds(pl.multiple_of(keep + j * CH, 8), CH)
        c = chunk[j]
        d1 = DEC[pl.ds(pl.multiple_of(HM - HB + keep + j * CH, 8), CH), :]
        D = d1
        for _ in range(1, G):
            D = D * d1
        r_own, r_other = R[mine, :], RP[c, :]
        first = jnp.where(p == 0, r_own, r_other)
        second = jnp.where(p == 0, r_other, r_own)

        @pl.when(has_pz)
        def _():
            forward[j].wait_recv()

        mid = D * EI[c, :] + first

        @pl.when(has_nz)
        def _():
            FW[c, :] = D * mid + second
            forward[j].start()

        @pl.when(p == 0)
        def _():
            DL[c, :] = mid
            deliver0[j].start()
            EN[mine, :] = EI[c, :]

        @pl.when(p == 1)
        def _():
            deliver1[j].start()
            EN[mine, :] = mid

    for j in range(CHUNKS):
        deliver0[j].wait_recv()
    EN[pl.ds(give, HALF), :] = EP[...]

    e = EN[...]
    outs = []
    F[0, fbig, :] = FIN[...] + e
    for g in range(G):
        e = dec * e + RES[g]
        fin = ENDS[g] + e
        OB[g, steps - 1] = fin[HB : HB + RL]
        if g + 1 < G:
            F[g + 1, fbig, :] = fin
    for g in range(G):
        c = pltpu.make_async_copy(OB.at[g, steps - 1], out.at[g, steps - 1], out_sem.at[g, steps - 1])
        c.start()
        outs.append(c)
    for m in range(steps - 1):
        for g in range(G):
            res, lo, n = phi(g, m, 2 * steps + 1 + m)
            if m < steps - 2:
                F[g, pl.ds(PAD + lo, n), :] = res
            OB[g, m] = res[HM - lo : HM - lo + RL]
            c = pltpu.make_async_copy(OB.at[g, m], out.at[g, m], out_sem.at[g, m])
            c.start()
            outs.append(c)
    for c in outs:
        c.wait()

    @pl.when(has_dn)
    def _():
        for c in down:
            c.wait_send()

    @pl.when(has_up)
    def _():
        for c in up:
            c.wait_send()

    @pl.when(has_next)
    def _():
        send_ends.wait_send()

    swap.wait_send()

    @pl.when(has_nz)
    def _():
        for c in forward:
            c.wait_send()

    for c in deliver0:
        c.wait_send()


def shards(cfg, sources, starts, coupling, classes, inverses, coarse_rate):
    G, RL, L = starts.shape
    steps = sources.shape[1]
    C, LB, _ = inverses.shape
    B = L // LB
    T = 3 * steps - 1
    HM = ceil8(T)
    NB = RL + 2 * ceil8(T - steps)
    HALF = NB // 2
    E = RL + 2 * HM
    f32, bf16 = jnp.float32, jnp.bfloat16
    dma = pltpu.SemaphoreType.DMA
    vm = pltpu.VMEM
    n_halo = 3 + steps
    return pl.pallas_call(
        functools.partial(kernel, cfg),
        out_shape=jax.ShapeDtypeStruct(sources.shape, f32),
        in_specs=[pl.BlockSpec(memory_space=pl.ANY)] * 2 + [pl.BlockSpec(memory_space=pltpu.VMEM)] * 4,
        out_specs=pl.BlockSpec(memory_space=pl.ANY),
        scratch_shapes=[
            vm((G, E + 2 * PAD, L), f32),
            vm((G, steps, E, L), f32),
            vm((2, 1, RL), f32),
            vm((2, B, RL), jnp.int32),
            vm((E, LB), f32),
            vm((B, C // 2, E, LB), bf16),
            vm((B, E, LB), f32),
            vm((3 * C // 2 * LB, 2 * LB), bf16),
            vm((NB, L), f32),
            vm((G, NB, L), f32),
            vm((G, NB, L), f32),
            vm((E, L), f32),
            vm((NB, L), f32),
            vm((HALF, L), f32),
            vm((HALF, L), f32),
            vm((HALF, L), f32),
            vm((NB, L), f32),
            vm((HALF, L), f32),
            vm((HALF, L), f32),
            vm((G, steps, RL, L), f32),
            dma((1 + steps,)),
            dma((2, n_halo)), dma((2, n_halo)),
            dma((1,)), dma((1,)),
            dma((1,)), dma((1,)),
            dma((CHUNKS,)), dma((CHUNKS,)),
            dma((CHUNKS,)), dma((CHUNKS,)),
            dma((G, steps)),
        ],
        compiler_params=pltpu.CompilerParams(
            collective_id=0, has_side_effects=True, vmem_limit_bytes=VMEM_LIMIT
        ),
        name="mgrit",
    )(sources, starts, coupling.reshape(1, RL), classes.T, inverses, coarse_rate)


def solution(mesh):
    in_specs = (
        P("tm", None, "space", None),
        P("tm", "space", None),
        P("space"),
        P("space", None),
        P(),
        P(),
    )
    cfg = (mesh.shape["tm"], mesh.shape["space"])
    body = functools.partial(shards, cfg)
    return jax.shard_map(
        body, mesh=mesh, in_specs=in_specs, out_specs=P("tm", None, "space", None), check_vma=False
    )
```

```python
import functools

import jax
import jax.numpy as jnp
from jax import lax
from jax.experimental import pallas as pl
from jax.experimental.pallas import tpu as pltpu
from jax.sharding import PartitionSpec as P

PAD = 8
CHUNKS = 9
VMEM_LIMIT = 16 * 1024 * 1024
MESH = pl.DeviceIdType.MESH


def ceil8(x):
    return -(-x // 8) * 8


def kernel(cfg, sources, starts, coupling_in, classes_in, inverses_in, rate_in, out,
           coupling, classes, inverses, rate, F, S, CPH, CLH, CP, MK, OD, W, FIN, ENDS, RES, DEC, R, RP, EI, EP, EN, FW, DL,
           in_sem, hs, hr, es, er, rs, rr, fs, fr, ps, pr):
    tm, space = cfg
    G, RL, L = starts.shape
    steps = sources.shape[1]
    C, LB, _ = inverses_in.shape
    B = L // LB
    KH = C // 2
    T = 3 * steps - 1
    HM = ceil8(T)
    HB = ceil8(T - steps)
    NB = RL + 2 * HB
    HALF = NB // 2
    CH = HALF // CHUNKS
    f32, bf16 = jnp.float32, jnp.bfloat16
    t = lax.axis_index("tm")
    s = lax.axis_index("space")
    p = lax.rem(t, 2)
    partner = t + 1 - 2 * p
    has_up, has_dn = s > 0, s < space - 1
    has_prev, has_next = t > 0, t < tm - 1
    has_pz, has_nz = t > 1, t < tm - 2

    small = [
        pltpu.make_async_copy(a, b, in_sem.at[1 + steps + i])
        for i, (a, b) in enumerate(
            [(inverses_in, inverses), (coupling_in, coupling), (classes_in, classes), (rate_in, rate)]
        )
    ]
    for c in small:
        c.start()
    own = pl.ds(HM, RL)
    in_starts = pltpu.make_async_copy(starts, F.at[:, pl.ds(PAD + HM, RL), :], in_sem.at[0])
    in_starts.start()
    in_src = [
        pltpu.make_async_copy(sources.at[:, m], S.at[:, m, own, :], in_sem.at[1 + m])
        for m in range(steps)
    ]
    for c in in_src:
        c.start()

    barrier = pltpu.get_barrier_semaphore()
    peers = [
        (has_up, (t, s - 1)), (has_dn, (t, s + 1)),
        (has_prev, (t - 1, s)), (has_next, (t + 1, s)),
        (has_pz, (t - 2, s)), (has_nz, (t + 2, s)),
    ]
    for cond, dev in peers:
        @pl.when(cond)
        def _(dev=dev):
            pl.semaphore_signal(barrier, inc=1, device_id=dev, device_id_type=MESH)
    pl.semaphore_wait(barrier, sum(jnp.where(cond, 1, 0) for cond, _ in peers))

    def remote(src, dst, a, b, dev):
        return pltpu.make_async_remote_copy(
            src_ref=src, dst_ref=dst, send_sem=a, recv_sem=b, device_id=dev, device_id_type=MESH
        )

    down, up = [], []
    halves = [HM if T - (m + 1) > HM - 8 else ceil8(T - (m + 1)) for m in range(steps)]
    down.append((coupling_in, CPH.at[0]))
    up.append((coupling_in, CPH.at[1]))
    down.append((classes_in, CLH.at[0]))
    up.append((classes_in, CLH.at[1]))
    order = [G - 1] + list(range(G - 1))
    needs = {}
    for g in order:
        needs[g, 0] = [len(down)]
        down.append((starts.at[g, pl.ds(RL - HM, HM), :], F.at[g, pl.ds(PAD, HM), :]))
        up.append((starts.at[g, pl.ds(0, HM), :], F.at[g, pl.ds(PAD + HM + RL, HM), :]))
        for m in range(steps):
            h = halves[m]
            needs.setdefault((g, m), []).append(len(down))
            down.append((sources.at[g, m, pl.ds(RL - h, h), :], S.at[g, m, pl.ds(HM - h, h), :]))
            up.append((sources.at[g, m, pl.ds(0, h), :], S.at[g, m, pl.ds(HM + RL, h), :]))
    down = [remote(a, b, hs.at[0, i], hr.at[0, i], (t, s + 1)) for i, (a, b) in enumerate(down)]
    up = [remote(a, b, hs.at[1, i], hr.at[1, i], (t, s - 1)) for i, (a, b) in enumerate(up)]

    @pl.when(has_dn)
    def _():
        for c in down:
            c.start()

    @pl.when(has_up)
    def _():
        for c in up:
            c.start()

    def clear(side):
        CPH[side] = jnp.zeros(CPH.shape[1:], f32)
        CLH[side] = jnp.zeros(CLH.shape[1:], jnp.int32)
        F[:, pl.ds(PAD + side * (HM + RL), HM), :] = jnp.zeros((G, HM, L), f32)
        S[:, :, pl.ds(side * (HM + RL), HM), :] = jnp.zeros((G, steps, HM, L), f32)

    @pl.when(jnp.logical_not(has_up))
    def _():
        clear(0)

    @pl.when(jnp.logical_not(has_dn))
    def _():
        clear(1)

    for g in range(G):
        F[g, pl.ds(0, PAD), :] = jnp.zeros((PAD, L), f32)
        F[g, pl.ds(PAD + HM * 2 + RL, PAD), :] = jnp.zeros((PAD, L), f32)

    for c in small:
        c.wait()

    for k in range(KH):
        for o in range(2):
            wt = inverses[2 * k + o].T
            hi = wt.astype(bf16)
            lo = (wt - hi.astype(f32)).astype(bf16)
            cols = pl.ds(o * LB, LB)
            W[pl.ds(k * LB, LB), cols] = hi
            W[pl.ds((KH + k) * LB, LB), cols] = hi
            W[pl.ds((2 * KH + k) * LB, LB), cols] = lo

    def column(row):
        return jnp.broadcast_to(row, (LB, RL)).T

    def fields(row, cls, part, n):
        for b in range(B):
            cl = column(cls[b : b + 1, :].astype(f32))[part]
            for k in range(KH):
                MK[b, k, pl.ds(row, n), :] = jnp.where((cl == 2 * k) | (cl == 2 * k + 1), 1.0, 0.0).astype(bf16)
            odd = cl == 1
            for k in range(1, KH):
                odd = odd | (cl == 2 * k + 1)
            OD[b, pl.ds(row, n), :] = jnp.where(odd, 1.0, 0.0)
            r = jnp.broadcast_to(rate[0:1, :], (n, LB))
            for c in range(1, C):
                r = jnp.where(cl == c, jnp.broadcast_to(rate[c : c + 1, :], (n, LB)), r)
            DEC[pl.ds(row, n), pl.ds(b * LB, LB)] = jnp.exp(-r)

    CP[own, :] = column(coupling[...])
    fields(HM, classes[...], slice(0, RL), RL)

    def arrived(which):
        @pl.when(has_up)
        def _():
            for i in which:
                down[i].wait_recv()

        @pl.when(has_dn)
        def _():
            for i in which:
                up[i].wait_recv()

    arrived([0, 1])
    CP[pl.ds(0, HM), :] = column(CPH[0])[RL - HM :]
    CP[pl.ds(HM + RL, HM), :] = column(CPH[1])[:HM]
    fields(0, CLH[0], slice(RL - HM, RL), HM)
    fields(HM + RL, CLH[1], slice(0, HM), HM)

    in_starts.wait()
    for c in in_src:
        c.wait()

    big = pl.ds(HM - HB, NB)
    fbig = pl.ds(PAD + HM - HB, NB)

    def phi(g, m, t_step):
        h = ceil8(T - t_step)
        lo, n = HM - h, RL + 2 * h
        xs = []
        for b in range(B):
            ln = pl.ds(b * LB, LB)
            v = F[g, pl.ds(PAD + lo, n), ln]
            a = F[g, pl.ds(PAD + lo - 1, n), ln]
            d = F[g, pl.ds(PAD + lo + 1, n), ln]
            rhs = v + CP[pl.ds(lo, n), :] * (a + d) + S[g, m, pl.ds(lo, n), ln]
            hi = rhs.astype(bf16)
            low = (rhs - hi.astype(f32)).astype(bf16)
            mk = [MK[b, k, pl.ds(lo, n), :] for k in range(KH)]
            his = [hi * q for q in mk]
            xs.append(jnp.concatenate(his + [low * q for q in mk] + his, axis=1))
        y = jnp.dot(jnp.concatenate(xs, axis=0), W[...], preferred_element_type=f32)
        res = []
        for b in range(B):
            odd = OD[b, pl.ds(lo, n), :] > 0.5
            yb = y[b * n : (b + 1) * n]
            res.append(jnp.where(odd, yb[:, LB:], yb[:, :LB]))
        return jnp.concatenate(res, axis=1), lo, n

    def relax(g, first, fresh=False):
        for m in range(steps - 1):
            if fresh:
                arrived(needs[g, m])
                if g == 0 and m == 0:
                    @pl.when(jnp.logical_not(has_prev))
                    def _():
                        FIN[...] = F[0, fbig, :]
            res, lo, n = phi(g, m, first + m)
            F[g, pl.ds(PAD + lo, n), :] = res

    send_ends = remote(ENDS.at[G - 1], FIN, es.at[0], er.at[0], (t + 1, s))
    for g in order:
        relax(g, 1, True)
        arrived(needs[g, steps - 1])
        res, lo, n = phi(g, steps - 1, steps)
        ENDS[g] = res
        if g == G - 1:
            @pl.when(has_next)
            def _():
                send_ends.start()

    for g in list(range(1, G)) + [0]:
        if g == 0:
            @pl.when(has_prev)
            def _():
                send_ends.wait_recv()
            F[g, fbig, :] = FIN[...]
        else:
            F[g, fbig, :] = ENDS[g - 1]
        relax(g, steps + 1)
        res, lo, n = phi(g, steps - 1, 2 * steps)
        RES[g] = res - ENDS[g]

    dec = DEC[big, :]
    acc = RES[0]
    for g in range(1, G):
        acc = dec * acc + RES[g]
    R[...] = acc
    keep = pl.multiple_of((1 - p) * HALF, 8)
    give = pl.multiple_of(p * HALF, 8)
    swap = [
        remote(R.at[pl.ds(pl.multiple_of(give + j * CH, 8), CH), :], RP.at[pl.ds(j * CH, CH)],
               rs.at[j], rr.at[j], (partner, s))
        for j in range(CHUNKS)
    ]
    for c in swap:
        c.start()

    @pl.when(jnp.logical_not(has_pz))
    def _():
        EI[...] = jnp.zeros((HALF, L), f32)

    chunk = [pl.ds(j * CH, CH) for j in range(CHUNKS)]
    forward = [remote(FW.at[c], EI.at[c], fs.at[j], fr.at[j], (t + 2, s)) for j, c in enumerate(chunk)]
    deliver0 = [remote(DL.at[c], EP.at[c], ps.at[j], pr.at[j], (partner, s)) for j, c in enumerate(chunk)]
    deliver1 = [remote(EI.at[c], EP.at[c], ps.at[j], pr.at[j], (partner, s)) for j, c in enumerate(chunk)]
    for j in range(CHUNKS):
        swap[j].wait_recv()
        mine = pl.ds(pl.multiple_of(keep + j * CH, 8), CH)
        c = chunk[j]
        d1 = DEC[pl.ds(pl.multiple_of(HM - HB + keep + j * CH, 8), CH), :]
        D = d1
        for _ in range(1, G):
            D = D * d1
        r_own, r_other = R[mine, :], RP[c, :]
        first = jnp.where(p == 0, r_own, r_other)
        second = jnp.where(p == 0, r_other, r_own)

        @pl.when(has_pz)
        def _():
            forward[j].wait_recv()

        mid = D * EI[c, :] + first

        @pl.when(has_nz)
        def _():
            FW[c, :] = D * mid + second
            forward[j].start()

        @pl.when(p == 0)
        def _():
            DL[c, :] = mid
            deliver0[j].start()
            EN[mine, :] = EI[c, :]

        @pl.when(p == 1)
        def _():
            deliver1[j].start()
            EN[mine, :] = mid

    for j in range(CHUNKS):
        deliver0[j].wait_recv()
    EN[pl.ds(give, HALF), :] = EP[...]

    e = EN[...]
    F[0, fbig, :] = FIN[...] + e
    for g in range(G):
        e = dec * e + RES[g]
        fin = ENDS[g] + e
        out[g, steps - 1] = fin[HB : HB + RL]
        if g + 1 < G:
            F[g + 1, fbig, :] = fin
    for m in range(steps - 1):
        for g in range(G):
            res, lo, n = phi(g, m, 2 * steps + 1 + m)
            if m < steps - 2:
                F[g, pl.ds(PAD + lo, n), :] = res
            out[g, m] = res[HM - lo : HM - lo + RL]

    @pl.when(has_dn)
    def _():
        for c in down:
            c.wait_send()

    @pl.when(has_up)
    def _():
        for c in up:
            c.wait_send()

    @pl.when(has_next)
    def _():
        send_ends.wait_send()

    for c in swap:
        c.wait_send()

    @pl.when(has_nz)
    def _():
        for c in forward:
            c.wait_send()

    for c in deliver0:
        c.wait_send()


def shards(cfg, sources, starts, coupling, classes, inverses, coarse_rate):
    G, RL, L = starts.shape
    steps = sources.shape[1]
    C, LB, _ = inverses.shape
    B = L // LB
    T = 3 * steps - 1
    HM = ceil8(T)
    NB = RL + 2 * ceil8(T - steps)
    HALF = NB // 2
    E = RL + 2 * HM
    f32, bf16 = jnp.float32, jnp.bfloat16
    dma = pltpu.SemaphoreType.DMA
    vm = pltpu.VMEM
    n_halo = 2 + G * (1 + steps)
    return pl.pallas_call(
        functools.partial(kernel, cfg),
        out_shape=jax.ShapeDtypeStruct(sources.shape, f32),
        in_specs=[pl.BlockSpec(memory_space=pltpu.HBM)] * 6,
        out_specs=pl.BlockSpec(memory_space=pltpu.VMEM),
        scratch_shapes=[
            vm((1, RL), f32),
            vm((B, RL), jnp.int32),
            vm((C, LB, LB), f32),
            vm((C, LB), f32),
            vm((G, E + 2 * PAD, L), f32),
            vm((G, steps, E, L), f32),
            vm((2, 1, RL), f32),
            vm((2, B, RL), jnp.int32),
            vm((E, LB), f32),
            vm((B, C // 2, E, LB), bf16),
            vm((B, E, LB), f32),
            vm((3 * C // 2 * LB, 2 * LB), bf16),
            vm((NB, L), f32),
            vm((G, NB, L), f32),
            vm((G, NB, L), f32),
            vm((E, L), f32),
            vm((NB, L), f32),
            vm((HALF, L), f32),
            vm((HALF, L), f32),
            vm((HALF, L), f32),
            vm((NB, L), f32),
            vm((HALF, L), f32),
            vm((HALF, L), f32),
            dma((5 + steps,)),
            dma((2, n_halo)), dma((2, n_halo)),
            dma((1,)), dma((1,)),
            dma((CHUNKS,)), dma((CHUNKS,)),
            dma((CHUNKS,)), dma((CHUNKS,)),
            dma((CHUNKS,)), dma((CHUNKS,)),
        ],
        compiler_params=pltpu.CompilerParams(
            collective_id=0, has_side_effects=True, vmem_limit_bytes=VMEM_LIMIT
        ),
        name="mgrit",
    )(*[
        pltpu.with_memory_space_constraint(a, pltpu.HBM)
        for a in (sources, starts, coupling.reshape(1, RL), classes.T, inverses, coarse_rate)
    ])


def solution(mesh):
    in_specs = (
        P("tm", None, "space", None),
        P("tm", "space", None),
        P("space"),
        P("space", None),
        P(),
        P(),
    )
    cfg = (mesh.shape["tm"], mesh.shape["space"])
    body = functools.partial(shards, cfg)
    return jax.shard_map(
        body, mesh=mesh, in_specs=in_specs, out_specs=P("tm", None, "space", None), check_vma=False
    )
```

```python
import functools

import jax
import jax.numpy as jnp
from jax import lax
from jax.experimental import pallas as pl
from jax.experimental.pallas import tpu as pltpu
from jax.sharding import PartitionSpec as P

PAD = 8
CHUNKS = 9
VMEM_LIMIT = 16 * 1024 * 1024
MESH = pl.DeviceIdType.MESH


def ceil8(x):
    return -(-x // 8) * 8


def kernel(cfg, sources, starts, coupling_in, classes_in, inverses_in, rate_in, out,
           coupling, classes, inverses, rate, F, S, CPH, CLH, CP, MK, OD, W, FIN, ENDS, RES, DEC, R, RP, RPB, QI, EI, EZ, EP, EN, FW, FW2, DL,
           in_sem, hs, hr, es, er, rs, rr, qs, qr, fs, fr, ps, pr):
    tm, space = cfg
    G, RL, L = starts.shape
    steps = sources.shape[1]
    C, LB, _ = inverses_in.shape
    B = L // LB
    KH = C // 2
    T = 3 * steps - 1
    HM = ceil8(T)
    HB = ceil8(T - steps)
    NB = RL + 2 * HB
    HALF = NB // 2
    CH = HALF // CHUNKS
    f32, bf16 = jnp.float32, jnp.bfloat16
    t = lax.axis_index("tm")
    s = lax.axis_index("space")
    p = lax.rem(t, 2)
    partner = t + 1 - 2 * p
    has_up, has_dn = s > 0, s < space - 1
    has_prev, has_next = t > 0, t < tm - 1
    has_pz, has_nz, has_nz2 = t > 1, t < tm - 2, t < tm - 4
    odd = lax.rem(t // 2, 2) == 1
    even = jnp.logical_not(odd)
    left, right = p == 0, p == 1

    small = [
        pltpu.make_async_copy(a, b, in_sem.at[1 + steps + i])
        for i, (a, b) in enumerate(
            [(inverses_in, inverses), (coupling_in, coupling), (classes_in, classes), (rate_in, rate)]
        )
    ]
    for c in small:
        c.start()
    own = pl.ds(HM, RL)
    in_starts = pltpu.make_async_copy(starts, F.at[:, pl.ds(PAD + HM, RL), :], in_sem.at[0])
    in_starts.start()
    in_src = [
        pltpu.make_async_copy(sources.at[:, m], S.at[:, m, own, :], in_sem.at[1 + m])
        for m in range(steps)
    ]
    for c in in_src:
        c.start()

    barrier = pltpu.get_barrier_semaphore()
    peers = [
        (has_up, (t, s - 1)), (has_dn, (t, s + 1)),
        (has_prev, (t - 1, s)), (has_next, (t + 1, s)),
        (has_pz, (t - 2, s)), (has_nz, (t + 2, s)),
        (t > 3, (t - 4, s)), (has_nz2, (t + 4, s)),
    ]
    for cond, dev in peers:
        @pl.when(cond)
        def _(dev=dev):
            pl.semaphore_signal(barrier, inc=1, device_id=dev, device_id_type=MESH)
    pl.semaphore_wait(barrier, sum(jnp.where(cond, 1, 0) for cond, _ in peers))

    def remote(src, dst, a, b, dev):
        return pltpu.make_async_remote_copy(
            src_ref=src, dst_ref=dst, send_sem=a, recv_sem=b, device_id=dev, device_id_type=MESH
        )

    down, up = [], []
    halves = [HM if T - (m + 1) > HM - 8 else ceil8(T - (m + 1)) for m in range(steps)]
    down.append((coupling_in, CPH.at[0]))
    up.append((coupling_in, CPH.at[1]))
    down.append((classes_in, CLH.at[0]))
    up.append((classes_in, CLH.at[1]))
    order = [G - 1] + list(range(G - 1))
    needs = {}
    for g in order:
        needs[g, 0] = [len(down)]
        down.append((starts.at[g, pl.ds(RL - HM, HM), :], F.at[g, pl.ds(PAD, HM), :]))
        up.append((starts.at[g, pl.ds(0, HM), :], F.at[g, pl.ds(PAD + HM + RL, HM), :]))
        for m in range(steps):
            h = halves[m]
            needs.setdefault((g, m), []).append(len(down))
            down.append((sources.at[g, m, pl.ds(RL - h, h), :], S.at[g, m, pl.ds(HM - h, h), :]))
            up.append((sources.at[g, m, pl.ds(0, h), :], S.at[g, m, pl.ds(HM + RL, h), :]))
    down = [remote(a, b, hs.at[0, i], hr.at[0, i], (t, s + 1)) for i, (a, b) in enumerate(down)]
    up = [remote(a, b, hs.at[1, i], hr.at[1, i], (t, s - 1)) for i, (a, b) in enumerate(up)]

    @pl.when(has_dn)
    def _():
        for c in down:
            c.start()

    @pl.when(has_up)
    def _():
        for c in up:
            c.start()

    def clear(side):
        CPH[side] = jnp.zeros(CPH.shape[1:], f32)
        CLH[side] = jnp.zeros(CLH.shape[1:], jnp.int32)
        F[:, pl.ds(PAD + side * (HM + RL), HM), :] = jnp.zeros((G, HM, L), f32)
        S[:, :, pl.ds(side * (HM + RL), HM), :] = jnp.zeros((G, steps, HM, L), f32)

    @pl.when(jnp.logical_not(has_up))
    def _():
        clear(0)

    @pl.when(jnp.logical_not(has_dn))
    def _():
        clear(1)

    for g in range(G):
        F[g, pl.ds(0, PAD), :] = jnp.zeros((PAD, L), f32)
        F[g, pl.ds(PAD + HM * 2 + RL, PAD), :] = jnp.zeros((PAD, L), f32)

    for c in small:
        c.wait()

    for k in range(KH):
        for o in range(2):
            wt = inverses[2 * k + o].T
            hi = wt.astype(bf16)
            lo = (wt - hi.astype(f32)).astype(bf16)
            cols = pl.ds(o * LB, LB)
            W[pl.ds(k * LB, LB), cols] = hi
            W[pl.ds((KH + k) * LB, LB), cols] = hi
            W[pl.ds((2 * KH + k) * LB, LB), cols] = lo

    def column(row):
        return jnp.broadcast_to(row, (LB, RL)).T

    def fields(row, cls, part, n):
        for b in range(B):
            cl = column(cls[b : b + 1, :].astype(f32))[part]
            for k in range(KH):
                MK[b, k, pl.ds(row, n), :] = jnp.where((cl == 2 * k) | (cl == 2 * k + 1), 1.0, 0.0).astype(bf16)
            odd = cl == 1
            for k in range(1, KH):
                odd = odd | (cl == 2 * k + 1)
            OD[b, pl.ds(row, n), :] = jnp.where(odd, 1.0, 0.0)
            r = jnp.broadcast_to(rate[0:1, :], (n, LB))
            for c in range(1, C):
                r = jnp.where(cl == c, jnp.broadcast_to(rate[c : c + 1, :], (n, LB)), r)
            DEC[pl.ds(row, n), pl.ds(b * LB, LB)] = jnp.exp(-r)

    CP[own, :] = column(coupling[...])
    fields(HM, classes[...], slice(0, RL), RL)

    def arrived(which):
        @pl.when(has_up)
        def _():
            for i in which:
                down[i].wait_recv()

        @pl.when(has_dn)
        def _():
            for i in which:
                up[i].wait_recv()

    arrived([0, 1])
    CP[pl.ds(0, HM), :] = column(CPH[0])[RL - HM :]
    CP[pl.ds(HM + RL, HM), :] = column(CPH[1])[:HM]
    fields(0, CLH[0], slice(RL - HM, RL), HM)
    fields(HM + RL, CLH[1], slice(0, HM), HM)

    in_starts.wait()
    for c in in_src:
        c.wait()

    big = pl.ds(HM - HB, NB)
    fbig = pl.ds(PAD + HM - HB, NB)

    def phi(g, m, t_step):
        h = ceil8(T - t_step)
        lo, n = HM - h, RL + 2 * h
        xs = []
        for b in range(B):
            ln = pl.ds(b * LB, LB)
            v = F[g, pl.ds(PAD + lo, n), ln]
            a = F[g, pl.ds(PAD + lo - 1, n), ln]
            d = F[g, pl.ds(PAD + lo + 1, n), ln]
            rhs = v + CP[pl.ds(lo, n), :] * (a + d) + S[g, m, pl.ds(lo, n), ln]
            hi = rhs.astype(bf16)
            low = (rhs - hi.astype(f32)).astype(bf16)
            mk = [MK[b, k, pl.ds(lo, n), :] for k in range(KH)]
            his = [hi * q for q in mk]
            xs.append(jnp.concatenate(his + [low * q for q in mk] + his, axis=1))
        y = jnp.dot(jnp.concatenate(xs, axis=0), W[...], preferred_element_type=f32)
        res = []
        for b in range(B):
            odd = OD[b, pl.ds(lo, n), :] > 0.5
            yb = y[b * n : (b + 1) * n]
            res.append(jnp.where(odd, yb[:, LB:], yb[:, :LB]))
        return jnp.concatenate(res, axis=1), lo, n

    def relax(g, first, fresh=False):
        for m in range(steps - 1):
            if fresh:
                arrived(needs[g, m])
                if g == 0 and m == 0:
                    @pl.when(jnp.logical_not(has_prev))
                    def _():
                        FIN[...] = F[0, fbig, :]
            res, lo, n = phi(g, m, first + m)
            F[g, pl.ds(PAD + lo, n), :] = res

    send_ends = remote(ENDS.at[G - 1], FIN, es.at[0], er.at[0], (t + 1, s))
    for g in order:
        relax(g, 1, True)
        arrived(needs[g, steps - 1])
        res, lo, n = phi(g, steps - 1, steps)
        ENDS[g] = res
        if g == G - 1:
            @pl.when(has_next)
            def _():
                send_ends.start()

    for g in list(range(1, G)) + [0]:
        if g == 0:
            @pl.when(has_prev)
            def _():
                send_ends.wait_recv()
            F[g, fbig, :] = FIN[...]
        else:
            F[g, fbig, :] = ENDS[g - 1]
        relax(g, steps + 1)
        res, lo, n = phi(g, steps - 1, 2 * steps)
        RES[g] = res - ENDS[g]

    dec = DEC[big, :]
    acc = RES[0]
    for g in range(1, G):
        acc = dec * acc + RES[g]
    R[...] = acc
    keep = pl.multiple_of((1 - p) * HALF, 8)
    give = pl.multiple_of(p * HALF, 8)
    chunk = [pl.ds(j * CH, CH) for j in range(CHUNKS)]

    def rows(base, j):
        return pl.ds(pl.multiple_of(base + j * CH, 8), CH)

    def copies(src, dst, a, b, dev, base=0):
        return [remote(src.at[rows(base, j)], dst.at[chunk[j]], a.at[j], b.at[j], dev)
                for j in range(CHUNKS)]

    def copies2(src, dst, a, b, dev, base, boff):
        return [remote(src.at[rows(base, j)], dst.at[chunk[j]], a.at[CHUNKS + j], b.at[boff + j], dev)
                for j in range(CHUNKS)]

    swap = copies(R, RP, rs, rr, (partner, s), give)
    swap2 = copies2(R, RPB, rs, rr, (partner, s), HALF, CHUNKS)
    pass_a = copies(FW, QI, qs, qr, (t + 2, s))
    pass_b = copies2(FW2, QI, qs, qr, (t + 1, s), 0, 0)
    far = copies(FW, EI, fs, fr, (t + 4, s))
    near = copies2(FW, EI, fs, fr, (t + 2, s), 0, 0)
    deliver0 = copies(DL, EP, ps, pr, (partner, s))
    deliver1 = copies(EZ, EP, ps, pr, (partner, s))

    @pl.when(left & even)
    def _():
        for c in swap2:
            c.start()

    @pl.when(left | odd)
    def _():
        for c in swap:
            c.start()

    def power(base, j):
        d1 = DEC[rows(base + HM - HB, j), :]
        D = d1
        for _ in range(1, G):
            D = D * d1
        return D

    @pl.when(right & even)
    def _():
        for j in range(CHUNKS):
            swap2[j].wait_recv()

            @pl.when(has_nz)
            def _():
                FW2[chunk[j], :] = power(HALF, j) * RPB[chunk[j], :] + R[rows(HALF, j), :]
                pass_b[j].start()

            swap[j].wait_recv()

            @pl.when(has_nz)
            def _():
                FW[chunk[j], :] = power(0, j) * RP[chunk[j], :] + R[rows(0, j), :]
                pass_a[j].start()

    @pl.when(odd)
    def _():
        for j in range(CHUNKS):
            swap[j].wait_recv()

    @pl.when(jnp.where(odd, t < 4, t < 2))
    def _():
        EI[...] = jnp.zeros((HALF, L), f32)

    for j in range(CHUNKS):
        mine = rows(keep, j)
        c = chunk[j]
        D = power(keep, j)

        @pl.when(jnp.where(odd, t > 3, t > 1))
        def _():
            far[j].wait_recv()

        @pl.when(odd)
        def _():
            pass_a[j].wait_recv()
            ez = D * (D * EI[c, :]) + QI[c, :]
            EZ[c, :] = ez
            r_own, r_other = R[mine, :], RP[c, :]

            @pl.when(has_nz)
            def _():
                first = jnp.where(left, r_own, r_other)
                second = jnp.where(left, r_other, r_own)
                FW[c, :] = D * (D * ez + first) + second
                near[j].start()

            @pl.when(has_nz2)
            def _():
                far[j].start()

        @pl.when(even)
        def _():
            EZ[c, :] = EI[c, :]

        @pl.when(left)
        def _():
            DL[c, :] = D * EZ[c, :] + R[mine, :]
            deliver0[j].start()
            EN[mine, :] = EZ[c, :]

        @pl.when(right)
        def _():
            deliver1[j].start()
            EN[mine, :] = D * EZ[c, :] + RP[c, :]

    for j in range(CHUNKS):
        deliver0[j].wait_recv()
    EN[pl.ds(give, HALF), :] = EP[...]

    e = EN[...]
    F[0, fbig, :] = FIN[...] + e
    for g in range(G):
        e = dec * e + RES[g]
        fin = ENDS[g] + e
        out[g, steps - 1] = fin[HB : HB + RL]
        if g + 1 < G:
            F[g + 1, fbig, :] = fin
    for m in range(steps - 1):
        for g in range(G):
            res, lo, n = phi(g, m, 2 * steps + 1 + m)
            if m < steps - 2:
                F[g, pl.ds(PAD + lo, n), :] = res
            out[g, m] = res[HM - lo : HM - lo + RL]

    @pl.when(has_dn)
    def _():
        for c in down:
            c.wait_send()

    @pl.when(has_up)
    def _():
        for c in up:
            c.wait_send()

    @pl.when(has_next)
    def _():
        send_ends.wait_send()

    def sent(cond, cs):
        @pl.when(cond)
        def _():
            for c in cs:
                c.wait_send()

    sent(left & even, swap2)
    sent(left | odd, swap)
    sent(right & even & has_nz, pass_a + pass_b)
    sent(odd & has_nz2, far)
    sent(odd & has_nz, near)
    for c in deliver0:
        c.wait_send()


def shards(cfg, sources, starts, coupling, classes, inverses, coarse_rate):
    G, RL, L = starts.shape
    steps = sources.shape[1]
    C, LB, _ = inverses.shape
    B = L // LB
    T = 3 * steps - 1
    HM = ceil8(T)
    NB = RL + 2 * ceil8(T - steps)
    HALF = NB // 2
    E = RL + 2 * HM
    f32, bf16 = jnp.float32, jnp.bfloat16
    dma = pltpu.SemaphoreType.DMA
    vm = pltpu.VMEM
    n_halo = 2 + G * (1 + steps)
    return pl.pallas_call(
        functools.partial(kernel, cfg),
        out_shape=jax.ShapeDtypeStruct(sources.shape, f32),
        in_specs=[pl.BlockSpec(memory_space=pltpu.HBM)] * 6,
        out_specs=pl.BlockSpec(memory_space=pltpu.VMEM),
        scratch_shapes=[
            vm((1, RL), f32),
            vm((B, RL), jnp.int32),
            vm((C, LB, LB), f32),
            vm((C, LB), f32),
            vm((G, E + 2 * PAD, L), f32),
            vm((G, steps, E, L), f32),
            vm((2, 1, RL), f32),
            vm((2, B, RL), jnp.int32),
            vm((E, LB), f32),
            vm((B, C // 2, E, LB), bf16),
            vm((B, E, LB), f32),
            vm((3 * C // 2 * LB, 2 * LB), bf16),
            vm((NB, L), f32),
            vm((G, NB, L), f32),
            vm((G, NB, L), f32),
            vm((E, L), f32),
            vm((NB, L), f32),
            *[vm((HALF, L), f32)] * 6,
            vm((NB, L), f32),
            *[vm((HALF, L), f32)] * 3,
            dma((5 + steps,)),
            dma((2, n_halo)), dma((2, n_halo)),
            dma((1,)), dma((1,)),
            dma((2 * CHUNKS,)), dma((2 * CHUNKS,)),
            dma((2 * CHUNKS,)), dma((CHUNKS,)),
            dma((2 * CHUNKS,)), dma((CHUNKS,)),
            dma((CHUNKS,)), dma((CHUNKS,)),
        ],
        compiler_params=pltpu.CompilerParams(
            collective_id=0, has_side_effects=True, vmem_limit_bytes=VMEM_LIMIT
        ),
        name="mgrit",
    )(*[
        pltpu.with_memory_space_constraint(a, pltpu.HBM)
        for a in (sources, starts, coupling.reshape(1, RL), classes.T, inverses, coarse_rate)
    ])


def solution(mesh):
    in_specs = (
        P("tm", None, "space", None),
        P("tm", "space", None),
        P("space"),
        P("space", None),
        P(),
        P(),
    )
    cfg = (mesh.shape["tm"], mesh.shape["space"])
    body = functools.partial(shards, cfg)
    return jax.shard_map(
        body, mesh=mesh, in_specs=in_specs, out_specs=P("tm", None, "space", None), check_vma=False
    )
```

```python
import functools

import jax
import jax.numpy as jnp
from jax import lax
from jax.experimental import pallas as pl
from jax.experimental.pallas import tpu as pltpu
from jax.sharding import PartitionSpec as P

PAD = 8
CHUNKS = 9
VMEM_LIMIT = 16 * 1024 * 1024
MESH = pl.DeviceIdType.MESH


def ceil8(x):
    return -(-x // 8) * 8


def kernel(cfg, sources, starts, coupling_in, classes_in, inverses_in, rate_in, out,
           coupling, classes, inverses, rate, F, S, CPH, CLH, CP, MK, OD, W, FIN, ENDS, RES, DEC, R, RP, QI, EI, EZ, EP, EN, FW, DL,
           in_sem, hs, hr, es, er, rs, rr, qs, qr, fs, fr, ps, pr):
    tm, space = cfg
    G, RL, L = starts.shape
    steps = sources.shape[1]
    C, LB, _ = inverses_in.shape
    B = L // LB
    KH = C // 2
    T = 3 * steps - 1
    HM = ceil8(T)
    HB = ceil8(T - steps)
    NB = RL + 2 * HB
    HALF = NB // 2
    CH = HALF // CHUNKS
    f32, bf16 = jnp.float32, jnp.bfloat16
    t = lax.axis_index("tm")
    s = lax.axis_index("space")
    p = lax.rem(t, 2)
    partner = t + 1 - 2 * p
    has_up, has_dn = s > 0, s < space - 1
    has_prev, has_next = t > 0, t < tm - 1
    has_pz, has_nz, has_nz2 = t > 1, t < tm - 2, t < tm - 4
    odd = lax.rem(t // 2, 2) == 1
    even = jnp.logical_not(odd)
    left, right = p == 0, p == 1

    small = [
        pltpu.make_async_copy(a, b, in_sem.at[1 + steps + i])
        for i, (a, b) in enumerate(
            [(inverses_in, inverses), (coupling_in, coupling), (classes_in, classes), (rate_in, rate)]
        )
    ]
    for c in small:
        c.start()
    own = pl.ds(HM, RL)
    in_starts = pltpu.make_async_copy(starts, F.at[:, pl.ds(PAD + HM, RL), :], in_sem.at[0])
    in_starts.start()
    in_src = [
        pltpu.make_async_copy(sources.at[:, m], S.at[:, m, own, :], in_sem.at[1 + m])
        for m in range(steps)
    ]
    for c in in_src:
        c.start()

    barrier = pltpu.get_barrier_semaphore()
    peers = [
        (has_up, (t, s - 1)), (has_dn, (t, s + 1)),
        (has_prev, (t - 1, s)), (has_next, (t + 1, s)),
        (has_pz, (t - 2, s)), (has_nz, (t + 2, s)),
        (t > 3, (t - 4, s)), (has_nz2, (t + 4, s)),
    ]
    for cond, dev in peers:
        @pl.when(cond)
        def _(dev=dev):
            pl.semaphore_signal(barrier, inc=1, device_id=dev, device_id_type=MESH)
    pl.semaphore_wait(barrier, sum(jnp.where(cond, 1, 0) for cond, _ in peers))

    def remote(src, dst, a, b, dev):
        return pltpu.make_async_remote_copy(
            src_ref=src, dst_ref=dst, send_sem=a, recv_sem=b, device_id=dev, device_id_type=MESH
        )

    down, up = [], []
    halves = [HM if T - (m + 1) > HM - 8 else ceil8(T - (m + 1)) for m in range(steps)]
    down.append((coupling_in, CPH.at[0]))
    up.append((coupling_in, CPH.at[1]))
    down.append((classes_in, CLH.at[0]))
    up.append((classes_in, CLH.at[1]))
    order = [G - 1] + list(range(G - 1))
    needs = {}
    for g in order:
        needs[g, 0] = [len(down)]
        down.append((starts.at[g, pl.ds(RL - HM, HM), :], F.at[g, pl.ds(PAD, HM), :]))
        up.append((starts.at[g, pl.ds(0, HM), :], F.at[g, pl.ds(PAD + HM + RL, HM), :]))
        for m in range(steps):
            h = halves[m]
            needs.setdefault((g, m), []).append(len(down))
            down.append((sources.at[g, m, pl.ds(RL - h, h), :], S.at[g, m, pl.ds(HM - h, h), :]))
            up.append((sources.at[g, m, pl.ds(0, h), :], S.at[g, m, pl.ds(HM + RL, h), :]))
    down = [remote(a, b, hs.at[0, i], hr.at[0, i], (t, s + 1)) for i, (a, b) in enumerate(down)]
    up = [remote(a, b, hs.at[1, i], hr.at[1, i], (t, s - 1)) for i, (a, b) in enumerate(up)]

    @pl.when(has_dn)
    def _():
        for c in down:
            c.start()

    @pl.when(has_up)
    def _():
        for c in up:
            c.start()

    def clear(side):
        CPH[side] = jnp.zeros(CPH.shape[1:], f32)
        CLH[side] = jnp.zeros(CLH.shape[1:], jnp.int32)
        F[:, pl.ds(PAD + side * (HM + RL), HM), :] = jnp.zeros((G, HM, L), f32)
        S[:, :, pl.ds(side * (HM + RL), HM), :] = jnp.zeros((G, steps, HM, L), f32)

    @pl.when(jnp.logical_not(has_up))
    def _():
        clear(0)

    @pl.when(jnp.logical_not(has_dn))
    def _():
        clear(1)

    for g in range(G):
        F[g, pl.ds(0, PAD), :] = jnp.zeros((PAD, L), f32)
        F[g, pl.ds(PAD + HM * 2 + RL, PAD), :] = jnp.zeros((PAD, L), f32)

    for c in small:
        c.wait()

    for k in range(KH):
        for o in range(2):
            wt = inverses[2 * k + o].T
            hi = wt.astype(bf16)
            lo = (wt - hi.astype(f32)).astype(bf16)
            cols = pl.ds(o * LB, LB)
            W[pl.ds(k * LB, LB), cols] = hi
            W[pl.ds((KH + k) * LB, LB), cols] = hi
            W[pl.ds((2 * KH + k) * LB, LB), cols] = lo

    def column(row):
        return jnp.broadcast_to(row, (LB, RL)).T

    def fields(row, cls, part, n):
        for b in range(B):
            cl = column(cls[b : b + 1, :].astype(f32))[part]
            for k in range(KH):
                MK[b, k, pl.ds(row, n), :] = jnp.where((cl == 2 * k) | (cl == 2 * k + 1), 1.0, 0.0).astype(bf16)
            odd = cl == 1
            for k in range(1, KH):
                odd = odd | (cl == 2 * k + 1)
            OD[b, pl.ds(row, n), :] = jnp.where(odd, 1.0, 0.0)
            r = jnp.broadcast_to(rate[0:1, :], (n, LB))
            for c in range(1, C):
                r = jnp.where(cl == c, jnp.broadcast_to(rate[c : c + 1, :], (n, LB)), r)
            DEC[pl.ds(row, n), pl.ds(b * LB, LB)] = jnp.exp(-r)

    CP[own, :] = column(coupling[...])
    fields(HM, classes[...], slice(0, RL), RL)

    def arrived(which):
        @pl.when(has_up)
        def _():
            for i in which:
                down[i].wait_recv()

        @pl.when(has_dn)
        def _():
            for i in which:
                up[i].wait_recv()

    arrived([0, 1])
    CP[pl.ds(0, HM), :] = column(CPH[0])[RL - HM :]
    CP[pl.ds(HM + RL, HM), :] = column(CPH[1])[:HM]
    fields(0, CLH[0], slice(RL - HM, RL), HM)
    fields(HM + RL, CLH[1], slice(0, HM), HM)

    in_starts.wait()
    for c in in_src:
        c.wait()

    big = pl.ds(HM - HB, NB)
    fbig = pl.ds(PAD + HM - HB, NB)

    def phi(g, m, t_step):
        h = ceil8(T - t_step)
        lo, n = HM - h, RL + 2 * h
        xs = []
        for b in range(B):
            ln = pl.ds(b * LB, LB)
            v = F[g, pl.ds(PAD + lo, n), ln]
            a = F[g, pl.ds(PAD + lo - 1, n), ln]
            d = F[g, pl.ds(PAD + lo + 1, n), ln]
            rhs = v + CP[pl.ds(lo, n), :] * (a + d) + S[g, m, pl.ds(lo, n), ln]
            hi = rhs.astype(bf16)
            low = (rhs - hi.astype(f32)).astype(bf16)
            mk = [MK[b, k, pl.ds(lo, n), :] for k in range(KH)]
            his = [hi * q for q in mk]
            xs.append(jnp.concatenate(his + [low * q for q in mk] + his, axis=1))
        y = jnp.dot(jnp.concatenate(xs, axis=0), W[...], preferred_element_type=f32)
        res = []
        for b in range(B):
            odd = OD[b, pl.ds(lo, n), :] > 0.5
            yb = y[b * n : (b + 1) * n]
            res.append(jnp.where(odd, yb[:, LB:], yb[:, :LB]))
        return jnp.concatenate(res, axis=1), lo, n

    def relax(g, first, fresh=False):
        for m in range(steps - 1):
            if fresh:
                arrived(needs[g, m])
                if g == 0 and m == 0:
                    @pl.when(jnp.logical_not(has_prev))
                    def _():
                        FIN[...] = F[0, fbig, :]
            res, lo, n = phi(g, m, first + m)
            F[g, pl.ds(PAD + lo, n), :] = res

    send_ends = remote(ENDS.at[G - 1], FIN, es.at[0], er.at[0], (t + 1, s))
    for g in order:
        relax(g, 1, True)
        arrived(needs[g, steps - 1])
        res, lo, n = phi(g, steps - 1, steps)
        ENDS[g] = res
        if g == G - 1:
            @pl.when(has_next)
            def _():
                send_ends.start()

    for g in list(range(1, G)) + [0]:
        if g == 0:
            @pl.when(has_prev)
            def _():
                send_ends.wait_recv()
            F[g, fbig, :] = FIN[...]
        else:
            F[g, fbig, :] = ENDS[g - 1]
        relax(g, steps + 1)
        res, lo, n = phi(g, steps - 1, 2 * steps)
        RES[g] = res - ENDS[g]

    dec = DEC[big, :]
    acc = RES[0]
    for g in range(1, G):
        acc = dec * acc + RES[g]
    R[...] = acc
    keep = pl.multiple_of((1 - p) * HALF, 8)
    give = pl.multiple_of(p * HALF, 8)
    chunk = [pl.ds(j * CH, CH) for j in range(CHUNKS)]

    def rows(base, j):
        return pl.ds(pl.multiple_of(base + j * CH, 8), CH)

    def copies(src, dst, a, b, dev, base=0):
        return [remote(src.at[rows(base, j)], dst.at[chunk[j]], a.at[j], b.at[j], dev)
                for j in range(CHUNKS)]

    swap = copies(R, RP, rs, rr, (partner, s), give)
    pass_a = copies(FW, QI, qs, qr, (t + 2, s))
    far = copies(FW, EI, fs, fr, (t + 4, s))
    near = [remote(FW.at[c], EI.at[c], fs.at[CHUNKS + j], fr.at[j], (t + 2, s)) for j, c in enumerate(chunk)]
    deliver0 = copies(DL, EP, ps, pr, (partner, s))
    deliver1 = copies(EZ, EP, ps, pr, (partner, s))

    for c in swap:
        c.start()

    def power(base, j):
        d1 = DEC[rows(base + HM - HB, j), :]
        D = d1
        for _ in range(1, G):
            D = D * d1
        return D

    def pair(j):
        r_own, r_other = R[rows(keep, j), :], RP[chunk[j], :]
        return jnp.where(left, r_own, r_other), jnp.where(left, r_other, r_own)

    for j in range(CHUNKS):
        swap[j].wait_recv()

        @pl.when(even & has_nz)
        def _():
            first, second = pair(j)
            FW[chunk[j], :] = power(keep, j) * first + second
            pass_a[j].start()

    @pl.when(jnp.where(odd, t < 4, t < 2))
    def _():
        EI[...] = jnp.zeros((HALF, L), f32)

    for j in range(CHUNKS):
        mine = rows(keep, j)
        c = chunk[j]
        D = power(keep, j)

        @pl.when(jnp.where(odd, t > 3, t > 1))
        def _():
            far[j].wait_recv()

        @pl.when(odd)
        def _():
            pass_a[j].wait_recv()
            ez = D * (D * EI[c, :]) + QI[c, :]
            EZ[c, :] = ez

            @pl.when(has_nz)
            def _():
                first, second = pair(j)
                FW[c, :] = D * (D * ez + first) + second

            @pl.when(has_nz2)
            def _():
                far[j].start()

            @pl.when(has_nz)
            def _():
                near[j].start()

        @pl.when(even)
        def _():
            EZ[c, :] = EI[c, :]

        @pl.when(left)
        def _():
            DL[c, :] = D * EZ[c, :] + R[mine, :]
            deliver0[j].start()
            EN[mine, :] = EZ[c, :]

        @pl.when(right)
        def _():
            deliver1[j].start()
            EN[mine, :] = D * EZ[c, :] + RP[c, :]

    for j in range(CHUNKS):
        deliver0[j].wait_recv()
    EN[pl.ds(give, HALF), :] = EP[...]

    e = EN[...]
    F[0, fbig, :] = FIN[...] + e
    for g in range(G):
        e = dec * e + RES[g]
        fin = ENDS[g] + e
        out[g, steps - 1] = fin[HB : HB + RL]
        if g + 1 < G:
            F[g + 1, fbig, :] = fin
    for m in range(steps - 1):
        for g in range(G):
            res, lo, n = phi(g, m, 2 * steps + 1 + m)
            if m < steps - 2:
                F[g, pl.ds(PAD + lo, n), :] = res
            out[g, m] = res[HM - lo : HM - lo + RL]

    @pl.when(has_dn)
    def _():
        for c in down:
            c.wait_send()

    @pl.when(has_up)
    def _():
        for c in up:
            c.wait_send()

    @pl.when(has_next)
    def _():
        send_ends.wait_send()

    def sent(cond, cs):
        @pl.when(cond)
        def _():
            for c in cs:
                c.wait_send()

    for c in swap:
        c.wait_send()
    sent(even & has_nz, pass_a)
    sent(odd & has_nz2, far)
    sent(odd & has_nz, near)
    for c in deliver0:
        c.wait_send()


def shards(cfg, sources, starts, coupling, classes, inverses, coarse_rate):
    G, RL, L = starts.shape
    steps = sources.shape[1]
    C, LB, _ = inverses.shape
    B = L // LB
    T = 3 * steps - 1
    HM = ceil8(T)
    NB = RL + 2 * ceil8(T - steps)
    HALF = NB // 2
    E = RL + 2 * HM
    f32, bf16 = jnp.float32, jnp.bfloat16
    dma = pltpu.SemaphoreType.DMA
    vm = pltpu.VMEM
    n_halo = 2 + G * (1 + steps)
    return pl.pallas_call(
        functools.partial(kernel, cfg),
        out_shape=jax.ShapeDtypeStruct(sources.shape, f32),
        in_specs=[pl.BlockSpec(memory_space=pltpu.HBM)] * 6,
        out_specs=pl.BlockSpec(memory_space=pltpu.VMEM),
        scratch_shapes=[
            vm((1, RL), f32),
            vm((B, RL), jnp.int32),
            vm((C, LB, LB), f32),
            vm((C, LB), f32),
            vm((G, E + 2 * PAD, L), f32),
            vm((G, steps, E, L), f32),
            vm((2, 1, RL), f32),
            vm((2, B, RL), jnp.int32),
            vm((E, LB), f32),
            vm((B, C // 2, E, LB), bf16),
            vm((B, E, LB), f32),
            vm((3 * C // 2 * LB, 2 * LB), bf16),
            vm((NB, L), f32),
            vm((G, NB, L), f32),
            vm((G, NB, L), f32),
            vm((E, L), f32),
            vm((NB, L), f32),
            *[vm((HALF, L), f32)] * 5,
            vm((NB, L), f32),
            *[vm((HALF, L), f32)] * 2,
            dma((5 + steps,)),
            dma((2, n_halo)), dma((2, n_halo)),
            dma((1,)), dma((1,)),
            dma((CHUNKS,)), dma((CHUNKS,)),
            dma((CHUNKS,)), dma((CHUNKS,)),
            dma((2 * CHUNKS,)), dma((CHUNKS,)),
            dma((CHUNKS,)), dma((CHUNKS,)),
        ],
        compiler_params=pltpu.CompilerParams(
            collective_id=0, has_side_effects=True, vmem_limit_bytes=VMEM_LIMIT
        ),
        name="mgrit",
    )(*[
        pltpu.with_memory_space_constraint(a, pltpu.HBM)
        for a in (sources, starts, coupling.reshape(1, RL), classes.T, inverses, coarse_rate)
    ])


def solution(mesh):
    in_specs = (
        P("tm", None, "space", None),
        P("tm", "space", None),
        P("space"),
        P("space", None),
        P(),
        P(),
    )
    cfg = (mesh.shape["tm"], mesh.shape["space"])
    body = functools.partial(shards, cfg)
    return jax.shard_map(
        body, mesh=mesh, in_specs=in_specs, out_specs=P("tm", None, "space", None), check_vma=False
    )
```
